32 devices in a mesh: ctx: 16 (over z, y, x), tp: 2 (over core).
Axes of the slice: x: 2, y: 2, z: 4, core: 2. Of those that a mesh axis runs over, the one named last changes fastest.
Arguments:
- ssm_input: bfloat16 [2048, 8192], P('ctx', 'tp'), may hold values from -40 to 40
- ssm_gate: bfloat16 [2048, 8192], P('ctx', 'tp'), may hold values from -4 to 4
- state_write: bfloat16 [2048, 128], P('ctx'), may hold values from -0.5 to 0.5
- state_read: bfloat16 [2048, 128], P('ctx'), may hold values from -0.5 to 0.5
- log_decay: float32 [2048, 32], P('ctx', 'tp'), may hold values from -4 to 0
- skip_gain: float32 [32], P('tp'), may hold values from 0.5 to 1.5
- norm_gain: float32 [8192], P('tp'), may hold values from 0.1 to 1.9
- ssm_cotangent: bfloat16 [2048, 8192], P('ctx', 'tp'), may hold values from -6 to 6
- queries: bfloat16 [2048, 8192], P('ctx', 'tp'), may hold values from -5 to 5
- key_states: bfloat16 [2048, 1024], P('ctx', 'tp'), may hold values from -5 to 5
- value_states: bfloat16 [2048, 1024], P('ctx', 'tp'), may hold values from -6 to 6
- attn_cotangent: bfloat16 [2048, 8192], P('ctx', 'tp'), may hold values from -6 to 6
Outputs:
- ssm_output: bfloat16 [2048, 8192], P('ctx', 'tp')
- input_grad: bfloat16 [2048, 8192], P('ctx', 'tp')
- gate_grad: bfloat16 [2048, 8192], P('ctx', 'tp')
- write_grad: float32 [2048, 128], P('ctx')
- read_grad: float32 [2048, 128], P('ctx')
- attn_output: bfloat16 [2048, 8192], P('ctx', 'tp')
- query_grad: bfloat16 [2048, 8192], P('ctx', 'tp')
- key_grad: bfloat16 [2048, 1024], P('ctx', 'tp')
- value_grad: bfloat16 [2048, 1024], P('ctx', 'tp')
The draws below stay inside these ranges and needn't reach their ends.
All inputs are finite; a program needn't handle non-finite values.
Results may differ from the reference program's by a relative error of at most 0.035.
Values may be sent and summed in bfloat16 or wider, within the bound.
A program may use at most 192 MiB of HBM per device.

```python
import math
from functools import partial
import jax
import jax.numpy as jnp
from jax import lax

STATE_HEADS = 32
P_SIZE = 256
NS = 128
QH = 64
KVH = 8
HD = 128
TOK_DEV = 128
HF = 64
TOKEN_COUNT = 2048
CH = 8192
N_CTX = 16


def draw_ssm_input(key, part):
    random_subkeys = jax.random.split(key, 3)
    column = jnp.arange(CH, dtype=jnp.float32) / CH
    col_scale = 0.5 * jnp.exp(math.log(3.0) * column + jax.random.uniform(random_subkeys[2], (CH,), minval=-0.7, maxval=0.7))
    base_draw = jnp.clip(jax.random.normal(random_subkeys[0], (TOKEN_COUNT, CH)), -4.0, 4.0)
    row_scale = jnp.exp(jax.random.uniform(random_subkeys[1], (TOKEN_COUNT, 1), minval=math.log(0.3), maxval=math.log(3.0)))
    return (base_draw * row_scale * col_scale[None, :]).astype(jnp.bfloat16)


def draw_log_decay(key, part):
    random_subkeys = jax.random.split(key, 7)
    order = jax.random.permutation(random_subkeys[0], STATE_HEADS)
    fast_heads = order < STATE_HEADS // 2
    fast_rate = jax.random.uniform(random_subkeys[1], (STATE_HEADS,), minval=2.0, maxval=3.0) / HF
    slow_rate = jnp.exp(jax.random.uniform(random_subkeys[2], (STATE_HEADS,), minval=math.log(1.0 / (16 * TOKEN_COUNT)), maxval=math.log(1.0 / (4 * TOKEN_COUNT))))
    decay_speed = jnp.where(fast_heads, fast_rate, slow_rate)
    coarse_estimate = jax.random.uniform(random_subkeys[3], (TOKEN_COUNT, STATE_HEADS), minval=0.5, maxval=2.0)
    block_draw = jax.random.uniform(random_subkeys[4], (TOKEN_COUNT // HF, STATE_HEADS), minval=0.5, maxval=2.0)
    block_multiplier = jnp.repeat(block_draw, HF, axis=0)
    spike_positions = jax.random.randint(random_subkeys[5], (3,), 0, TOKEN_COUNT)
    spike_rows = jnp.any(jnp.arange(TOKEN_COUNT)[:, None] == spike_positions[None, :], axis=1)
    spike_loss = jnp.log(jax.random.uniform(random_subkeys[6], (TOKEN_COUNT, STATE_HEADS), minval=0.5, maxval=0.8))
    return -decay_speed[None, :] * coarse_estimate * block_multiplier + jnp.where(spike_rows[:, None], spike_loss, 0.0)


def draw_queries(key, part):
    return jnp.clip(jax.random.normal(jax.random.fold_in(key, 11), (TOKEN_COUNT, QH * HD)), -4.0, 4.0).astype(jnp.bfloat16)


def draw_key_states(key, part):
    return jnp.clip(jax.random.normal(jax.random.fold_in(key, 13), (TOKEN_COUNT, KVH * HD)), -4.0, 4.0).astype(jnp.bfloat16)


def block_scale(own_key, dims, cuts, smallest, high):
    def one(axis_at, shards_of):
        steps = jax.random.uniform(jax.random.fold_in(jax.random.fold_in(own_key, 6), axis_at), (shards_of,), jnp.float32, smallest / len(cuts), high / len(cuts))
        return jnp.repeat(jnp.exp(steps), dims[axis_at] // shards_of).reshape((-1,) + (1,) * (len(dims) - axis_at - 1))

    factor_of = one(*cuts[0])
    for cut in cuts[1:]:
        factor_of = factor_of * one(*cut)
    return factor_of


def gaussian(stream_key, shape, deviation, bound, cuts=(), kind=jnp.bfloat16):
    result = jax.random.normal(stream_key, shape, jnp.float32) * deviation
    if len(cuts) > 0:
        result = block_scale(stream_key, shape, cuts, -0.22, 0.18) * result
    return jnp.clip(result, min=-bound, max=bound).astype(kind)


def setup_inputs(seed: int = 0) -> dict:
    arg_keys = jax.random.split(jax.random.key(seed), 13)
    ssm_input = draw_ssm_input(jax.random.fold_in(arg_keys[12], 71), 0)
    ssm_gate = gaussian(arg_keys[1], (TOKEN_COUNT, CH), 1.0, 4.0, ((0, 16), (1, 2)))
    state_write = gaussian(arg_keys[2], (TOKEN_COUNT, NS), NS ** -0.5, 0.5, ((0, 16),))
    state_read = gaussian(arg_keys[3], (TOKEN_COUNT, NS), NS ** -0.5, 0.5, ((0, 16),))
    log_decay = draw_log_decay(jax.random.fold_in(arg_keys[12], 71), 0)
    skip_gain = jnp.clip(0.5 + 1.0 * jax.random.uniform(arg_keys[5], (STATE_HEADS,), jnp.float32) ** block_scale(arg_keys[5], (STATE_HEADS,), ((0, 2),), -0.2, 0.2), 0.5, 1.5)
    norm_gain = jnp.clip(1.0 + 0.18 * jax.random.normal(arg_keys[6], (CH,), jnp.float32), 0.1, 1.9)
    ssm_cotangent = gaussian(arg_keys[7], (TOKEN_COUNT, CH), 1.0, 6.0, ((0, 16), (1, 2)))
    queries = draw_queries(jax.random.fold_in(arg_keys[12], 71), 0)
    key_states = draw_key_states(jax.random.fold_in(arg_keys[12], 71), 0)
    value_states = gaussian(arg_keys[10], (TOKEN_COUNT, KVH * HD), 1.0, 6.0, ((0, 16), (1, 2)))
    attn_cotangent = gaussian(arg_keys[11], (TOKEN_COUNT, QH * HD), 1.0, 6.0, ((0, 16), (1, 2)))
    return dict(ssm_input=ssm_input, ssm_gate=ssm_gate, state_write=state_write, state_read=state_read, log_decay=log_decay, skip_gain=skip_gain, norm_gain=norm_gain, ssm_cotangent=ssm_cotangent, queries=queries, key_states=key_states, value_states=value_states, attn_cotangent=attn_cotangent)


PRECISE = lax.Precision.HIGHEST
NEGATIVE = -1e+30
EPSILON = 1e-05

def sequence_rows():
    position = jnp.arange(TOKEN_COUNT, dtype=jnp.int32)
    block_id = position // HF
    device_id = jnp.where(block_id < N_CTX, block_id, 2 * N_CTX - 1 - block_id)
    second = jnp.where(block_id < N_CTX, 0, 1)
    return (device_id * TOK_DEV + second * HF + position % HF).astype(jnp.int32)

def folded_rows():
    row_id = jnp.arange(TOKEN_COUNT, dtype=jnp.int32)
    device_id = row_id // TOK_DEV
    local_id = row_id % TOK_DEV
    block_id = jnp.where(local_id < HF, device_id, 2 * N_CTX - 1 - device_id)
    return (block_id * HF + local_id % HF).astype(jnp.int32)

def block_step(zero_state, pieces):
    input_block, write_block, read_block, decay_block = pieces
    log_total = jnp.cumsum(decay_block, axis=0)
    log_gap = log_total[:, None, :] - log_total[None, :, :]
    causal = jnp.arange(HF)[:, None] >= jnp.arange(HF)[None, :]
    decay = jnp.exp(jnp.where(causal[:, :, None], log_gap, NEGATIVE))
    read_write = jnp.dot(read_block, write_block.T, precision=PRECISE)
    weights = decay * read_write[:, :, None]
    mixed = jnp.einsum('tsh,shp->thp', weights, input_block, precision=PRECISE)
    mixed = mixed + jnp.exp(log_total)[:, :, None] * jnp.einsum('hpn,tn->thp', zero_state, read_block, precision=PRECISE)
    log_last = log_total[-1]
    shrink = jnp.exp(log_last[None, :] - log_total)
    new_state = jnp.exp(log_last)[:, None, None] * zero_state + jnp.einsum('shp,sn->hpn', shrink[:, :, None] * input_block, write_block, precision=PRECISE)
    return (new_state, mixed)

def ssm_map(input_seq, gate_seq, write_seq, read_seq, decay_seq, skip_gain, norm_gain):
    blocks = 2 * N_CTX
    initial = jnp.zeros((STATE_HEADS, P_SIZE, NS), dtype=input_seq.dtype)
    pieces = (input_seq.reshape(blocks, HF, STATE_HEADS, P_SIZE), write_seq.reshape(blocks, HF, NS), read_seq.reshape(blocks, HF, NS), decay_seq.reshape(blocks, HF, STATE_HEADS))
    _, mixed = lax.scan(block_step, initial, pieces)
    mixed = mixed.reshape(TOKEN_COUNT, STATE_HEADS, P_SIZE) + skip_gain[None, :, None] * input_seq.reshape(TOKEN_COUNT, STATE_HEADS, P_SIZE)
    gated = mixed.reshape(TOKEN_COUNT, CH) * jax.nn.silu(gate_seq)
    root_mean = jnp.sqrt(lax.optimization_barrier(jnp.mean(gated * gated, axis=1, keepdims=True)) + EPSILON)
    return gated / root_mean * norm_gain

def head_terms(pieces, causal, score_scale):
    query_head, key_head, value_head, cot_head = pieces
    scores = jnp.dot(query_head, key_head.T, preferred_element_type=jnp.float32) * score_scale
    scores = jnp.where(causal, scores, NEGATIVE)
    row_max = lax.optimization_barrier(jnp.max(scores, axis=1, keepdims=True))
    log_norm = row_max + jnp.log(lax.optimization_barrier(jnp.sum(jnp.exp(scores - row_max), axis=1, keepdims=True)))
    probs_full = jnp.exp(scores - log_norm)
    weights = probs_full.astype(jnp.bfloat16)
    output = jnp.dot(weights, value_head, preferred_element_type=jnp.float32).astype(jnp.bfloat16)
    delta_row = lax.optimization_barrier(jnp.sum(cot_head.astype(jnp.float32) * output.astype(jnp.float32), axis=1, keepdims=True))
    d_prob = jnp.dot(cot_head, value_head.T, preferred_element_type=jnp.float32)
    d_score = (probs_full * (d_prob - delta_row) * score_scale).astype(jnp.bfloat16)
    query_g = jnp.dot(d_score, key_head, preferred_element_type=jnp.float32).astype(jnp.bfloat16)
    key_g = jnp.dot(d_score.T, query_head, preferred_element_type=jnp.float32)
    value_g = jnp.dot(weights.T, cot_head, preferred_element_type=jnp.float32)
    return (output, query_g, key_g, value_g)

def reference(ssm_input, ssm_gate, state_write, state_read, log_decay, skip_gain, norm_gain, ssm_cotangent, queries, key_states, value_states, attn_cotangent):
    to_seq = sequence_rows()
    to_fold = folded_rows()

    def ordered(values):
        return jnp.take(values, to_seq, axis=0)

    def folded(values):
        return jnp.take(values, to_fold, axis=0)
    decay_seq = ordered(log_decay).astype(jnp.float32)

    def ssm_local(input_seq, gate_seq, write_seq, read_seq):
        return ssm_map(input_seq, gate_seq, write_seq, read_seq, decay_seq, skip_gain, norm_gain)
    primal = (ordered(ssm_input).astype(jnp.float32), ordered(ssm_gate).astype(jnp.float32), ordered(state_write).astype(jnp.float32), ordered(state_read).astype(jnp.float32))
    ssm_seq, pullback = jax.vjp(ssm_local, *primal)
    input_g, gate_g, write_g, read_g = pullback(ordered(ssm_cotangent).astype(jnp.float32))
    ssm_output = folded(ssm_seq).astype(jnp.bfloat16)
    input_grad = folded(input_g).astype(jnp.bfloat16)
    gate_grad = folded(gate_g).astype(jnp.bfloat16)
    write_grad = folded(write_g).astype(jnp.float32)
    read_grad = folded(read_g).astype(jnp.float32)
    group_size = QH // KVH
    query_heads = jnp.transpose(ordered(queries).reshape(TOKEN_COUNT, QH, HD), (1, 0, 2))
    cot_heads = jnp.transpose(ordered(attn_cotangent).reshape(TOKEN_COUNT, QH, HD), (1, 0, 2))
    key_heads = jnp.repeat(jnp.transpose(ordered(key_states).reshape(TOKEN_COUNT, KVH, HD), (1, 0, 2)), group_size, axis=0)
    value_heads = jnp.repeat(jnp.transpose(ordered(value_states).reshape(TOKEN_COUNT, KVH, HD), (1, 0, 2)), group_size, axis=0)
    causal = jnp.arange(TOKEN_COUNT)[:, None] >= jnp.arange(TOKEN_COUNT)[None, :]
    outputs, query_g, key_g, value_g = lax.map(partial(head_terms, causal=causal, score_scale=HD ** (-0.5)), (query_heads, key_heads, value_heads, cot_heads))
    attn_output = folded(jnp.transpose(outputs, (1, 0, 2)).reshape(TOKEN_COUNT, QH * HD))
    query_grad = folded(jnp.transpose(query_g, (1, 0, 2)).reshape(TOKEN_COUNT, QH * HD))
    key_sum = lax.optimization_barrier(jnp.sum(key_g.reshape(KVH, group_size, TOKEN_COUNT, HD), axis=1))
    value_sum = lax.optimization_barrier(jnp.sum(value_g.reshape(KVH, group_size, TOKEN_COUNT, HD), axis=1))
    key_grad = folded(jnp.transpose(key_sum, (1, 0, 2)).reshape(TOKEN_COUNT, KVH * HD)).astype(jnp.bfloat16)
    value_grad = folded(jnp.transpose(value_sum, (1, 0, 2)).reshape(TOKEN_COUNT, KVH * HD)).astype(jnp.bfloat16)
    return (ssm_output, input_grad, gate_grad, write_grad, read_grad, attn_output, query_grad, key_grad, value_grad)
```

```python
import functools

import jax
import jax.numpy as jnp
from jax import lax
from jax.experimental import pallas as pl
from jax.experimental.pallas import tpu as pltpu
from jax.sharding import PartitionSpec as P

HD = 128
CH = 8192
PRECISE = lax.Precision.HIGHEST
NEGATIVE = -1e30
EPSILON = 1e-05
TILE_KEYS = 256
CHUNK = 256
VMEM_BYTES = 48 * 1024 * 1024


def dot(a, b, a_dim, b_dim):
    return lax.dot_general(
        a, b, (((a_dim,), (b_dim,)), ((), ())), preferred_element_type=jnp.float32
    )


def attention_kernel(
    place_ref, q_ref, kv_ref, cot_ref, out_ref, dq_ref, dkv_ref,
    keys, values, dk_sum, dv_sum, scores, q_rows, cot_rows, acc,
):
    count, _, _, half_rows, _ = kv_ref.shape
    group = q_ref.shape[1] // HD
    rows = group * half_rows
    scale = HD ** (-0.5)
    place = place_ref[0]
    for j in range(count):
        near = pl.ds(j * half_rows, half_rows)
        far = pl.ds((2 * count - 1 - j) * half_rows, half_rows)
        keys[near] = kv_ref[j, 0, 0]
        keys[far] = kv_ref[j, 0, 1]
        values[near] = kv_ref[j, 1, 0]
        values[far] = kv_ref[j, 1, 1]
    dk_sum[...] = jnp.zeros_like(dk_sum)
    dv_sum[...] = jnp.zeros_like(dv_sum)
    for half in range(2):
        block = place if half == 0 else 2 * count - 1 - place
        tiles = block // (TILE_KEYS // half_rows) + 1
        for h in range(group):
            there = (pl.ds(half * half_rows, half_rows), pl.ds(h * HD, HD))
            q_rows[pl.ds(h * half_rows, half_rows)] = q_ref[there]
            cot_rows[pl.ds(h * half_rows, half_rows)] = cot_ref[there]
        q_pos = block * half_rows + lax.broadcasted_iota(jnp.int32, (1, rows), 1) % half_rows

        def score_turn(tile, top):
            at = pl.ds(pl.multiple_of(tile * TILE_KEYS, TILE_KEYS), TILE_KEYS)
            s = dot(keys[at], q_rows[...], 1, 1) * scale
            key_pos = tile * TILE_KEYS + lax.broadcasted_iota(jnp.int32, s.shape, 0)
            s = jnp.where(key_pos <= q_pos, s, NEGATIVE)
            scores[at] = s
            return jnp.maximum(top, jnp.max(s, axis=0, keepdims=True))

        top = lax.fori_loop(0, tiles, score_turn, jnp.full((1, rows), NEGATIVE, jnp.float32))
        acc[...] = jnp.zeros_like(acc)

        def value_turn(tile, total):
            at = pl.ds(pl.multiple_of(tile * TILE_KEYS, TILE_KEYS), TILE_KEYS)
            p = jnp.exp(scores[at] - top)
            scores[at] = p
            acc[...] += dot(values[at], p.astype(jnp.bfloat16), 0, 0)
            return total + jnp.sum(p, axis=0, keepdims=True)

        total = lax.fori_loop(0, tiles, value_turn, jnp.zeros((1, rows), jnp.float32))
        inverse = 1.0 / total
        out_t = acc[...] * inverse
        out_rows = out_t.T.astype(jnp.bfloat16)
        cot_t = cot_rows[...].astype(jnp.float32).T
        delta = jnp.sum(
            cot_t * out_t.astype(jnp.bfloat16).astype(jnp.float32), axis=0, keepdims=True
        )
        acc[...] = jnp.zeros_like(acc)

        def grad_turn(tile, carry):
            at = pl.ds(pl.multiple_of(tile * TILE_KEYS, TILE_KEYS), TILE_KEYS)
            w = scores[at] * inverse
            d_prob = dot(values[at], cot_rows[...], 1, 1)
            d_score = (w * (d_prob - delta) * scale).astype(jnp.bfloat16)
            acc[...] += dot(keys[at], d_score, 0, 0)
            dk_sum[at] += dot(d_score, q_rows[...], 1, 0)
            dv_sum[at] += dot(w.astype(jnp.bfloat16), cot_rows[...], 1, 0)
            return carry

        lax.fori_loop(0, tiles, grad_turn, 0)
        dq_rows = acc[...].T.astype(jnp.bfloat16)
        for h in range(group):
            there = (pl.ds(half * half_rows, half_rows), pl.ds(h * HD, HD))
            out_ref[there] = out_rows[h * half_rows : (h + 1) * half_rows]
            dq_ref[there] = dq_rows[h * half_rows : (h + 1) * half_rows]
    for j in range(count):
        near = pl.ds(j * half_rows, half_rows)
        far = pl.ds((2 * count - 1 - j) * half_rows, half_rows)
        dkv_ref[j, 0, 0] = dk_sum[near].astype(jnp.bfloat16)
        dkv_ref[j, 0, 1] = dk_sum[far].astype(jnp.bfloat16)
        dkv_ref[j, 1, 0] = dv_sum[near].astype(jnp.bfloat16)
        dkv_ref[j, 1, 1] = dv_sum[far].astype(jnp.bfloat16)


def attention_core(queries, kv_all, attn_cotangent, place):
    tok_rows, q_cols = queries.shape
    count, _, _, half_rows, kv_cols = kv_all.shape
    kv_heads = kv_cols // HD
    width = q_cols // kv_heads
    rows = width // HD * half_rows
    total = count * tok_rows
    wide = pl.BlockSpec((tok_rows, width), lambda g, place: (0, g))
    pair = pl.BlockSpec((count, 2, 2, half_rows, HD), lambda g, place: (0, 0, 0, 0, g))
    like_q = jax.ShapeDtypeStruct(queries.shape, jnp.bfloat16)
    flops = 7 * 2 * tok_rows * q_cols * total // 2
    return pl.pallas_call(
        attention_kernel,
        out_shape=(like_q, like_q, jax.ShapeDtypeStruct(kv_all.shape, jnp.bfloat16)),
        grid_spec=pltpu.PrefetchScalarGridSpec(
            num_scalar_prefetch=1,
            grid=(kv_heads,),
            in_specs=[wide, pair, wide],
            out_specs=(wide, wide, pair),
            scratch_shapes=[
                pltpu.VMEM((total, HD), jnp.bfloat16),
                pltpu.VMEM((total, HD), jnp.bfloat16),
                pltpu.VMEM((total, HD), jnp.float32),
                pltpu.VMEM((total, HD), jnp.float32),
                pltpu.VMEM((total, rows), jnp.float32),
                pltpu.VMEM((rows, HD), jnp.bfloat16),
                pltpu.VMEM((rows, HD), jnp.bfloat16),
                pltpu.VMEM((HD, rows), jnp.float32),
            ],
        ),
        compiler_params=pltpu.CompilerParams(vmem_limit_bytes=VMEM_BYTES),
        cost_estimate=pl.CostEstimate(
            flops=3 * flops, bytes_accessed=16 * 1024 * 1024, transcendentals=total * q_cols // 2
        ),
        name="attention_both",
    )(place.reshape(1).astype(jnp.int32), queries, kv_all, attn_cotangent)


def attention(queries, key_states, value_states, attn_cotangent):
    tok_rows = queries.shape[0]
    half_rows = tok_rows // 2
    kv_cols = key_states.shape[1]
    count = lax.axis_size("ctx")
    kv = jnp.stack([key_states, value_states])
    kv_all = lax.all_gather(kv, "ctx", axis=0).reshape(count, 2, 2, half_rows, kv_cols)
    attn_output, query_grad, dkv = attention_core(
        queries, kv_all, attn_cotangent, lax.axis_index("ctx")
    )
    mine = lax.psum_scatter(
        dkv.reshape(count, 2, tok_rows, kv_cols), "ctx", scatter_dimension=0, tiled=False
    )
    return (attn_output, query_grad, mine[0], mine[1])


def in_order(ref, step, steps):
    pieces = ref.shape[0]
    early = step < steps // 2
    return [ref[jnp.where(early, j, pieces - 1 - j)] for j in range(pieces)]


def put_in_order(ref, value, step, steps):
    pieces, rows = ref.shape[0], ref.shape[1]
    early = step < steps // 2
    for j in range(pieces):
        ref[jnp.where(early, j, pieces - 1 - j)] = value[j * rows : (j + 1) * rows].astype(
            ref.dtype
        )


def whole(ref, step, steps):
    return jnp.concatenate(in_order(ref, step, steps), axis=0)


def causal_decay(col, row, flip):
    shape = (col.shape[0], row.shape[1])
    down = lax.broadcasted_iota(jnp.int32, shape, 0)
    across = lax.broadcasted_iota(jnp.int32, shape, 1)
    if flip:
        return jnp.exp(jnp.where(across >= down, row - col, NEGATIVE))
    return jnp.exp(jnp.where(down >= across, col - row, NEGATIVE))


def forward_kernel(steps, x_ref, b_ref, c_ref, col_ref, row_ref, mixed_ref, state_ref, state):
    step = pl.program_id(0)

    @pl.when(step == 0)
    def _():
        state[...] = jnp.zeros_like(state)

    x = whole(x_ref, step, steps)
    b = whole(b_ref, step, steps)
    c = whole(c_ref, step, steps)
    col, row = col_ref[...], row_ref[0]
    last = col[CHUNK - 1 : CHUNK]
    weights = (causal_decay(col, row, False) * dot(c, b, 1, 1)).astype(jnp.bfloat16)
    entering = state[...]
    entering_short = entering.astype(jnp.bfloat16)
    state_ref[0] = entering_short
    mixed = dot(weights, x, 1, 0) + jnp.exp(col) * dot(c, entering_short, 1, 0)
    put_in_order(mixed_ref, mixed, step, steps)
    shrunk = (b.astype(jnp.float32) * jnp.exp(last - col)).astype(jnp.bfloat16)
    state[...] = jnp.exp(last) * entering + dot(shrunk, x, 0, 0)


def backward_kernel(
    steps, x_ref, dm_ref, b_ref, c_ref, col_ref, row_ref, state_ref,
    input_ref, maps_ref, adjoint,
):
    step = steps - 1 - pl.program_id(0)

    @pl.when(pl.program_id(0) == 0)
    def _():
        adjoint[...] = jnp.zeros_like(adjoint)

    x = whole(x_ref, step, steps)
    dm = whole(dm_ref, step, steps)
    b = whole(b_ref, step, steps)
    c = whole(c_ref, step, steps)
    col, row = col_ref[...], row_ref[0]
    last = col[CHUNK - 1 : CHUNK]
    shrink, grow = jnp.exp(last - col), jnp.exp(col)
    entering = adjoint[...]
    entering_short = entering.astype(jnp.bfloat16)
    decay_t = causal_decay(col, row, True)
    weights_t = (decay_t * dot(b, c, 1, 1)).astype(jnp.bfloat16)
    input_g = dot(weights_t, dm, 1, 0) + shrink * dot(b, entering_short, 1, 0)
    put_in_order(input_ref, input_g, step, steps)
    pairs_t = (decay_t * dot(x, dm, 1, 1)).astype(jnp.bfloat16)
    write_g = dot(pairs_t, c, 1, 0) + shrink * dot(x, entering_short, 1, 1)
    pairs = (causal_decay(col, row, False) * dot(dm, x, 1, 1)).astype(jnp.bfloat16)
    read_g = dot(pairs, b, 1, 0) + grow * dot(dm, state_ref[0], 1, 1)
    put_in_order(maps_ref, jnp.concatenate([write_g, read_g], axis=1), step, steps)
    grown = (c.astype(jnp.float32) * grow).astype(jnp.bfloat16)
    adjoint[...] = jnp.exp(last) * entering + dot(grown, dm, 0, 0)


def ssm_specs(count, half_rows, steps, order):
    per = CHUNK // half_rows

    def rows_spec(cols):
        def place(i):
            step = order(i)
            early = step < steps // 2
            return (
                jnp.where(early, step, steps - 1 - step), jnp.where(early, 0, 1), 0, 0
            )

        return pl.BlockSpec((per, pl.Squeezed(), half_rows, cols), place)

    return (
        rows_spec,
        pl.BlockSpec((CHUNK, 1), lambda i: (order(i), 0)),
        pl.BlockSpec((1, 1, CHUNK), lambda i: (order(i), 0, 0)),
    )


def scan_forward(x, b, c, col, row):
    count, _, half_rows, cols = x.shape
    states = b.shape[-1]
    steps = count * 2 * half_rows // CHUNK
    rows_spec, col_spec, row_spec = ssm_specs(count, half_rows, steps, lambda i: i)
    return pl.pallas_call(
        functools.partial(forward_kernel, steps),
        grid=(steps,),
        in_specs=[rows_spec(cols), rows_spec(states), rows_spec(states), col_spec, row_spec],
        out_specs=(rows_spec(cols), pl.BlockSpec((1, states, cols), lambda i: (i, 0, 0))),
        out_shape=(
            jax.ShapeDtypeStruct(x.shape, jnp.bfloat16),
            jax.ShapeDtypeStruct((steps, states, cols), jnp.bfloat16),
        ),
        scratch_shapes=[pltpu.VMEM((states, cols), jnp.float32)],
        compiler_params=pltpu.CompilerParams(vmem_limit_bytes=VMEM_BYTES),
        cost_estimate=pl.CostEstimate(
            flops=8 * 10**9, bytes_accessed=8 * 1024 * 1024, transcendentals=10**6
        ),
        name="scan_forward",
    )(x, b, c, col, row)


def scan_backward(x, dm, b, c, col, row, state):
    count, _, half_rows, cols = x.shape
    states = b.shape[-1]
    steps = count * 2 * half_rows // CHUNK
    rows_spec, col_spec, row_spec = ssm_specs(
        count, half_rows, steps, lambda i: steps - 1 - i
    )
    return pl.pallas_call(
        functools.partial(backward_kernel, steps),
        grid=(steps,),
        in_specs=[
            rows_spec(cols), rows_spec(cols), rows_spec(states), rows_spec(states),
            col_spec, row_spec,
            pl.BlockSpec((1, states, cols), lambda i: (steps - 1 - i, 0, 0)),
        ],
        out_specs=(rows_spec(cols), rows_spec(2 * states)),
        out_shape=(
            jax.ShapeDtypeStruct(x.shape, jnp.bfloat16),
            jax.ShapeDtypeStruct((count, 2, half_rows, 2 * states), jnp.bfloat16),
        ),
        scratch_shapes=[pltpu.VMEM((states, cols), jnp.float32)],
        compiler_params=pltpu.CompilerParams(vmem_limit_bytes=VMEM_BYTES),
        cost_estimate=pl.CostEstimate(
            flops=16 * 10**9, bytes_accessed=12 * 1024 * 1024, transcendentals=2 * 10**6
        ),
        name="scan_backward",
    )(x, dm, b, c, col, row, state)


def to_channels(values):
    return lax.all_to_all(values, "ctx", split_axis=1, concat_axis=0, tiled=True)


def to_tokens(values):
    return lax.all_to_all(values, "ctx", split_axis=0, concat_axis=1, tiled=True)


def ssm_layer(
    ssm_input, ssm_gate, state_write, state_read, log_decay, skip_gain, norm_gain, ssm_cotangent
):
    tok_rows, channel_count = ssm_input.shape
    head_count = log_decay.shape[1]
    half_rows = tok_rows // 2
    head_dim = channel_count // head_count
    count = lax.axis_size("ctx")
    own_cols = channel_count // count
    states = state_write.shape[1]
    folded = (count, 2, half_rows)
    x_all = to_channels(ssm_input).reshape(*folded, own_cols)
    b_all = lax.all_gather(state_write, "ctx", axis=0).reshape(*folded, states)
    c_all = lax.all_gather(state_read, "ctx", axis=0).reshape(*folded, states)
    decay_all = lax.all_gather(log_decay, "ctx", axis=0).reshape(*folded, head_count)
    head = lax.axis_index("ctx") * own_cols // head_dim
    own_decay = lax.dynamic_index_in_dim(decay_all, head, 3, False)
    ordered = jnp.concatenate([own_decay[:, 0], own_decay[::-1, 1]]).reshape(-1, CHUNK)
    upto = jnp.triu(jnp.ones((CHUNK, CHUNK), jnp.float32))
    log_total = jnp.dot(ordered, upto, precision=PRECISE)
    col = log_total.reshape(-1, 1)
    row = log_total[:, None, :]
    mixed_all, state_all = scan_forward(x_all, b_all, c_all, col, row)
    skip = jnp.repeat(skip_gain, head_dim)[None, :]
    mixed = to_tokens(mixed_all.reshape(count * tok_rows, own_cols)).astype(jnp.float32)
    mixed = mixed + skip * ssm_input.astype(jnp.float32)
    gate = ssm_gate.astype(jnp.float32)
    sigmoid = jax.nn.sigmoid(gate)
    gated = mixed * gate * sigmoid
    d_normed = ssm_cotangent.astype(jnp.float32) * norm_gain
    sums = lax.psum(
        jnp.stack([jnp.sum(gated * gated, axis=1), jnp.sum(d_normed * gated, axis=1)]), "tp"
    )
    root_mean = jnp.sqrt(sums[0] / CH + EPSILON)[:, None]
    inner_mean = (sums[1] / CH)[:, None] / root_mean
    normed = gated / root_mean
    ssm_output = (normed * norm_gain).astype(jnp.bfloat16)
    d_gated = (d_normed - normed * inner_mean) / root_mean
    d_mixed = d_gated * gate * sigmoid
    gate_grad = (d_gated * mixed * sigmoid * (1.0 + gate * (1.0 - sigmoid))).astype(jnp.bfloat16)
    dm_all = to_channels(d_mixed.astype(jnp.bfloat16)).reshape(*folded, own_cols)
    input_all, maps_all = scan_backward(x_all, dm_all, b_all, c_all, col, row, state_all)
    input_g = to_tokens(input_all.reshape(count * tok_rows, own_cols)).astype(jnp.float32)
    input_grad = (input_g + skip * d_mixed).astype(jnp.bfloat16)
    maps = lax.psum_scatter(
        maps_all.reshape(count, tok_rows, 2 * states), "ctx", scatter_dimension=0, tiled=False
    )
    maps = lax.psum(maps, "tp").astype(jnp.float32)
    return (ssm_output, input_grad, gate_grad, maps[:, :states], maps[:, states:])


def per_device(
    ssm_input,
    ssm_gate,
    state_write,
    state_read,
    log_decay,
    skip_gain,
    norm_gain,
    ssm_cotangent,
    queries,
    key_states,
    value_states,
    attn_cotangent,
):
    ssm_results = ssm_layer(
        ssm_input, ssm_gate, state_write, state_read, log_decay, skip_gain, norm_gain, ssm_cotangent
    )
    attn_results = attention(queries, key_states, value_states, attn_cotangent)
    return ssm_results + attn_results


def solution(mesh):
    placed = (
        P("ctx", "tp"),
        P("ctx", "tp"),
        P("ctx", None),
        P("ctx", None),
        P("ctx", "tp"),
        P("tp"),
        P("tp"),
        P("ctx", "tp"),
        P("ctx", "tp"),
        P("ctx", "tp"),
        P("ctx", "tp"),
        P("ctx", "tp"),
    )
    return jax.shard_map(
        per_device,
        mesh=mesh,
        in_specs=placed,
        out_specs=(
            P("ctx", "tp"),
            P("ctx", "tp"),
            P("ctx", "tp"),
            P("ctx", None),
            P("ctx", None),
            P("ctx", "tp"),
            P("ctx", "tp"),
            P("ctx", "tp"),
            P("ctx", "tp"),
        ),
        check_vma=False,
    )
```

```python
import functools

import jax
import jax.numpy as jnp
from jax import lax
from jax.experimental import pallas as pl
from jax.experimental.pallas import tpu as pltpu
from jax.sharding import PartitionSpec as P

HD = 128
CH = 8192
PRECISE = lax.Precision.HIGHEST
NEGATIVE = -1e30
EPSILON = 1e-05
TILE_KEYS = 256
CHUNK = 256
VMEM_BYTES = 48 * 1024 * 1024


def dot(a, b, a_dim, b_dim):
    return lax.dot_general(
        a, b, (((a_dim,), (b_dim,)), ((), ())), preferred_element_type=jnp.float32
    )


def attention_kernel(
    place_ref, q_ref, kv_ref, cot_ref, out_ref, dq_ref, dkv_ref,
    keys, values, dk_sum, dv_sum, scores, q_rows, cot_rows, acc,
):
    count, _, _, half_rows, _ = kv_ref.shape
    group = q_ref.shape[1] // HD
    rows = group * half_rows
    scale = HD ** (-0.5)
    place = place_ref[0]
    for j in range(count):
        near = pl.ds(j * half_rows, half_rows)
        far = pl.ds((2 * count - 1 - j) * half_rows, half_rows)
        keys[near] = kv_ref[j, 0, 0]
        keys[far] = kv_ref[j, 0, 1]
        values[near] = kv_ref[j, 1, 0]
        values[far] = kv_ref[j, 1, 1]
    dk_sum[...] = jnp.zeros_like(dk_sum)
    dv_sum[...] = jnp.zeros_like(dv_sum)
    for half in range(2):
        block = place if half == 0 else 2 * count - 1 - place
        tiles = block // (TILE_KEYS // half_rows) + 1
        for h in range(group):
            there = (pl.ds(half * half_rows, half_rows), pl.ds(h * HD, HD))
            q_rows[pl.ds(h * half_rows, half_rows)] = q_ref[there]
            cot_rows[pl.ds(h * half_rows, half_rows)] = cot_ref[there]
        q_pos = block * half_rows + lax.broadcasted_iota(jnp.int32, (1, rows), 1) % half_rows

        def score_turn(tile, top):
            at = pl.ds(pl.multiple_of(tile * TILE_KEYS, TILE_KEYS), TILE_KEYS)
            s = dot(keys[at], q_rows[...], 1, 1) * scale
            key_pos = tile * TILE_KEYS + lax.broadcasted_iota(jnp.int32, s.shape, 0)
            s = jnp.where(key_pos <= q_pos, s, NEGATIVE)
            scores[at] = s
            return jnp.maximum(top, jnp.max(s, axis=0, keepdims=True))

        top = lax.fori_loop(0, tiles, score_turn, jnp.full((1, rows), NEGATIVE, jnp.float32))
        acc[...] = jnp.zeros_like(acc)

        def value_turn(tile, total):
            at = pl.ds(pl.multiple_of(tile * TILE_KEYS, TILE_KEYS), TILE_KEYS)
            p = jnp.exp(scores[at] - top)
            scores[at] = p
            acc[...] += dot(values[at], p.astype(jnp.bfloat16), 0, 0)
            return total + jnp.sum(p, axis=0, keepdims=True)

        total = lax.fori_loop(0, tiles, value_turn, jnp.zeros((1, rows), jnp.float32))
        inverse = 1.0 / total
        out_t = acc[...] * inverse
        out_rows = out_t.T.astype(jnp.bfloat16)
        cot_t = cot_rows[...].astype(jnp.float32).T
        delta = jnp.sum(
            cot_t * out_t.astype(jnp.bfloat16).astype(jnp.float32), axis=0, keepdims=True
        )
        acc[...] = jnp.zeros_like(acc)

        def grad_turn(tile, carry):
            at = pl.ds(pl.multiple_of(tile * TILE_KEYS, TILE_KEYS), TILE_KEYS)
            w = scores[at] * inverse
            d_prob = dot(values[at], cot_rows[...], 1, 1)
            d_score = (w * (d_prob - delta) * scale).astype(jnp.bfloat16)
            acc[...] += dot(keys[at], d_score, 0, 0)
            dk_sum[at] += dot(d_score, q_rows[...], 1, 0)
            dv_sum[at] += dot(w.astype(jnp.bfloat16), cot_rows[...], 1, 0)
            return carry

        lax.fori_loop(0, tiles, grad_turn, 0)
        dq_rows = acc[...].T.astype(jnp.bfloat16)
        for h in range(group):
            there = (pl.ds(half * half_rows, half_rows), pl.ds(h * HD, HD))
            out_ref[there] = out_rows[h * half_rows : (h + 1) * half_rows]
            dq_ref[there] = dq_rows[h * half_rows : (h + 1) * half_rows]
    for j in range(count):
        near = pl.ds(j * half_rows, half_rows)
        far = pl.ds((2 * count - 1 - j) * half_rows, half_rows)
        dkv_ref[j, 0, 0] = dk_sum[near].astype(jnp.bfloat16)
        dkv_ref[j, 0, 1] = dk_sum[far].astype(jnp.bfloat16)
        dkv_ref[j, 1, 0] = dv_sum[near].astype(jnp.bfloat16)
        dkv_ref[j, 1, 1] = dv_sum[far].astype(jnp.bfloat16)


def attention_core(queries, kv_all, attn_cotangent, place):
    tok_rows, q_cols = queries.shape
    count, _, _, half_rows, kv_cols = kv_all.shape
    kv_heads = kv_cols // HD
    width = q_cols // kv_heads
    rows = width // HD * half_rows
    total = count * tok_rows
    wide = pl.BlockSpec((tok_rows, width), lambda g, place: (0, g))
    pair = pl.BlockSpec((count, 2, 2, half_rows, HD), lambda g, place: (0, 0, 0, 0, g))
    like_q = jax.ShapeDtypeStruct(queries.shape, jnp.bfloat16)
    flops = 7 * 2 * tok_rows * q_cols * total // 2
    return pl.pallas_call(
        attention_kernel,
        out_shape=(like_q, like_q, jax.ShapeDtypeStruct(kv_all.shape, jnp.bfloat16)),
        grid_spec=pltpu.PrefetchScalarGridSpec(
            num_scalar_prefetch=1,
            grid=(kv_heads,),
            in_specs=[wide, pair, wide],
            out_specs=(wide, wide, pair),
            scratch_shapes=[
                pltpu.VMEM((total, HD), jnp.bfloat16),
                pltpu.VMEM((total, HD), jnp.bfloat16),
                pltpu.VMEM((total, HD), jnp.float32),
                pltpu.VMEM((total, HD), jnp.float32),
                pltpu.VMEM((total, rows), jnp.float32),
                pltpu.VMEM((rows, HD), jnp.bfloat16),
                pltpu.VMEM((rows, HD), jnp.bfloat16),
                pltpu.VMEM((HD, rows), jnp.float32),
            ],
        ),
        compiler_params=pltpu.CompilerParams(vmem_limit_bytes=VMEM_BYTES),
        cost_estimate=pl.CostEstimate(
            flops=3 * flops, bytes_accessed=16 * 1024 * 1024, transcendentals=total * q_cols // 2
        ),
        name="attention_both",
    )(place.reshape(1).astype(jnp.int32), queries, kv_all, attn_cotangent)


def gather_pair(key_states, value_states):
    tok_rows, kv_cols = key_states.shape
    kv = jnp.stack([key_states, value_states])
    return lax.all_gather(kv, "ctx", axis=0).reshape(
        lax.axis_size("ctx"), 2, 2, tok_rows // 2, kv_cols
    )


def scatter_pair(dkv):
    count, _, _, half_rows, kv_cols = dkv.shape
    mine = lax.psum_scatter(
        dkv.reshape(count, 2, 2 * half_rows, kv_cols), "ctx", scatter_dimension=0, tiled=False
    )
    return (mine[0], mine[1])


def in_order(ref, step, steps):
    pieces = ref.shape[0]
    early = step < steps // 2
    return [ref[jnp.where(early, j, pieces - 1 - j)] for j in range(pieces)]


def put_in_order(ref, value, step, steps):
    pieces, rows = ref.shape[0], ref.shape[1]
    early = step < steps // 2
    for j in range(pieces):
        ref[jnp.where(early, j, pieces - 1 - j)] = value[j * rows : (j + 1) * rows].astype(
            ref.dtype
        )


def whole(ref, step, steps):
    return jnp.concatenate(in_order(ref, step, steps), axis=0)


def causal_decay(col, row, flip):
    shape = (col.shape[0], row.shape[1])
    down = lax.broadcasted_iota(jnp.int32, shape, 0)
    across = lax.broadcasted_iota(jnp.int32, shape, 1)
    if flip:
        return jnp.exp(jnp.where(across >= down, row - col, NEGATIVE))
    return jnp.exp(jnp.where(down >= across, col - row, NEGATIVE))


def forward_kernel(steps, x_ref, b_ref, c_ref, col_ref, row_ref, mixed_ref, state_ref, state):
    step = pl.program_id(0)

    @pl.when(step == 0)
    def _():
        state[...] = jnp.zeros_like(state)

    x = whole(x_ref, step, steps)
    b = whole(b_ref, step, steps)
    c = whole(c_ref, step, steps)
    col, row = col_ref[...], row_ref[0]
    last = col[CHUNK - 1 : CHUNK]
    weights = (causal_decay(col, row, False) * dot(c, b, 1, 1)).astype(jnp.bfloat16)
    entering = state[...]
    entering_short = entering.astype(jnp.bfloat16)
    state_ref[0] = entering_short
    mixed = dot(weights, x, 1, 0) + jnp.exp(col) * dot(c, entering_short, 1, 0)
    put_in_order(mixed_ref, mixed, step, steps)
    shrunk = (b.astype(jnp.float32) * jnp.exp(last - col)).astype(jnp.bfloat16)
    state[...] = jnp.exp(last) * entering + dot(shrunk, x, 0, 0)


def backward_kernel(
    steps, x_ref, dm_ref, b_ref, c_ref, col_ref, row_ref, state_ref,
    input_ref, write_ref, read_ref, adjoint,
):
    step = steps - 1 - pl.program_id(0)

    @pl.when(pl.program_id(0) == 0)
    def _():
        adjoint[...] = jnp.zeros_like(adjoint)

    x = whole(x_ref, step, steps)
    dm = whole(dm_ref, step, steps)
    b = whole(b_ref, step, steps)
    c = whole(c_ref, step, steps)
    col, row = col_ref[...], row_ref[0]
    last = col[CHUNK - 1 : CHUNK]
    shrink, grow = jnp.exp(last - col), jnp.exp(col)
    entering = adjoint[...]
    entering_short = entering.astype(jnp.bfloat16)
    decay_t = causal_decay(col, row, True)
    weights_t = (decay_t * dot(b, c, 1, 1)).astype(jnp.bfloat16)
    input_g = dot(weights_t, dm, 1, 0) + shrink * dot(b, entering_short, 1, 0)
    put_in_order(input_ref, input_g, step, steps)
    pairs_t = (decay_t * dot(x, dm, 1, 1)).astype(jnp.bfloat16)
    write_g = dot(pairs_t, c, 1, 0) + shrink * dot(x, entering_short, 1, 1)
    pairs = (causal_decay(col, row, False) * dot(dm, x, 1, 1)).astype(jnp.bfloat16)
    read_g = dot(pairs, b, 1, 0) + grow * dot(dm, state_ref[0], 1, 1)
    put_in_order(write_ref, write_g, step, steps)
    put_in_order(read_ref, read_g, step, steps)
    grown = (c.astype(jnp.float32) * grow).astype(jnp.bfloat16)
    adjoint[...] = jnp.exp(last) * entering + dot(grown, dm, 0, 0)


def ssm_specs(count, half_rows, steps, order):
    per = CHUNK // half_rows

    def rows_spec(cols):
        def place(i):
            step = order(i)
            early = step < steps // 2
            return (
                jnp.where(early, step, steps - 1 - step), jnp.where(early, 0, 1), 0, 0
            )

        return pl.BlockSpec((per, pl.Squeezed(), half_rows, cols), place)

    return (
        rows_spec,
        pl.BlockSpec((CHUNK, 1), lambda i: (order(i), 0)),
        pl.BlockSpec((1, 1, CHUNK), lambda i: (order(i), 0, 0)),
    )


def scan_forward(x, b, c, col, row):
    count, _, half_rows, cols = x.shape
    states = b.shape[-1]
    steps = count * 2 * half_rows // CHUNK
    rows_spec, col_spec, row_spec = ssm_specs(count, half_rows, steps, lambda i: i)
    return pl.pallas_call(
        functools.partial(forward_kernel, steps),
        grid=(steps,),
        in_specs=[rows_spec(cols), rows_spec(states), rows_spec(states), col_spec, row_spec],
        out_specs=(rows_spec(cols), pl.BlockSpec((1, states, cols), lambda i: (i, 0, 0))),
        out_shape=(
            jax.ShapeDtypeStruct(x.shape, jnp.bfloat16),
            jax.ShapeDtypeStruct((steps, states, cols), jnp.bfloat16),
        ),
        scratch_shapes=[pltpu.VMEM((states, cols), jnp.float32)],
        compiler_params=pltpu.CompilerParams(vmem_limit_bytes=VMEM_BYTES),
        cost_estimate=pl.CostEstimate(
            flops=8 * 10**9, bytes_accessed=8 * 1024 * 1024, transcendentals=10**6
        ),
        name="scan_forward",
    )(x, b, c, col, row)


def scan_backward(x, dm, b, c, col, row, state):
    count, _, half_rows, cols = x.shape
    states = b.shape[-1]
    steps = count * 2 * half_rows // CHUNK
    rows_spec, col_spec, row_spec = ssm_specs(
        count, half_rows, steps, lambda i: steps - 1 - i
    )
    return pl.pallas_call(
        functools.partial(backward_kernel, steps),
        grid=(steps,),
        in_specs=[
            rows_spec(cols), rows_spec(cols), rows_spec(states), rows_spec(states),
            col_spec, row_spec,
            pl.BlockSpec((1, states, cols), lambda i: (steps - 1 - i, 0, 0)),
        ],
        out_specs=(rows_spec(cols), rows_spec(states), rows_spec(states)),
        out_shape=(
            jax.ShapeDtypeStruct(x.shape, jnp.bfloat16),
            jax.ShapeDtypeStruct(b.shape, jnp.bfloat16),
            jax.ShapeDtypeStruct(b.shape, jnp.bfloat16),
        ),
        scratch_shapes=[pltpu.VMEM((states, cols), jnp.float32)],
        compiler_params=pltpu.CompilerParams(vmem_limit_bytes=VMEM_BYTES),
        cost_estimate=pl.CostEstimate(
            flops=16 * 10**9, bytes_accessed=12 * 1024 * 1024, transcendentals=2 * 10**6
        ),
        name="scan_backward",
    )(x, dm, b, c, col, row, state)


def to_channels(values, extra=None):
    count = lax.axis_size("ctx")
    parts = values.reshape(values.shape[0], count, -1)
    if extra is not None:
        shape = (values.shape[0], count, extra.shape[1])
        parts = jnp.concatenate([parts, jnp.broadcast_to(extra[:, None, :], shape)], axis=2)
    blocks = jnp.transpose(parts, (1, 0, 2))
    return lax.all_to_all(blocks, "ctx", split_axis=0, concat_axis=0)


def to_owners(blocks):
    return lax.all_to_all(blocks, "ctx", split_axis=0, concat_axis=0)


def side_by_side(blocks):
    return jnp.transpose(blocks, (1, 0, 2)).reshape(blocks.shape[1], -1)


def from_other_core(values):
    return lax.ppermute(values, "tp", [(0, 1), (1, 0)])


def both_layers(
    ssm_input, ssm_gate, state_write, state_read, log_decay, skip_gain, norm_gain, ssm_cotangent,
    queries, key_states, value_states, attn_cotangent,
):
    tok_rows, channel_count = ssm_input.shape
    head_count = log_decay.shape[1]
    half_rows = tok_rows // 2
    head_dim = channel_count // head_count
    count = lax.axis_size("ctx")
    own_cols = channel_count // count
    states = state_write.shape[1]
    folded = (count, 2, half_rows)
    share_maps = lax.axis_size("tp") == 2
    kv_all = gather_pair(key_states, value_states)
    if share_maps:
        first = lax.axis_index("tp") == 0
        arrived = to_channels(ssm_input, jnp.where(first, state_write, state_read))
        own_map = arrived[:, :, own_cols:]
        other_map = from_other_core(own_map)
        b_all = jnp.where(first, own_map, other_map).reshape(*folded, states)
        c_all = jnp.where(first, other_map, own_map).reshape(*folded, states)
    else:
        arrived = to_channels(ssm_input, jnp.concatenate([state_write, state_read], axis=1))
        b_all = arrived[:, :, own_cols : own_cols + states].reshape(*folded, states)
        c_all = arrived[:, :, own_cols + states :].reshape(*folded, states)
    x_all = arrived[:, :, :own_cols].reshape(*folded, own_cols)
    decay_rows = jnp.repeat(log_decay.T, head_dim // own_cols, axis=0)
    own_decay = to_owners(decay_rows[:, None, :]).reshape(*folded)
    ordered = jnp.concatenate([own_decay[:, 0], own_decay[::-1, 1]]).reshape(-1, CHUNK)
    upto = jnp.triu(jnp.ones((CHUNK, CHUNK), jnp.float32))
    log_total = jnp.dot(ordered, upto, precision=PRECISE)
    col = log_total.reshape(-1, 1)
    row = log_total[:, None, :]
    mixed_all, state_all = scan_forward(x_all, b_all, c_all, col, row)
    skip = jnp.repeat(skip_gain, head_dim)[None, :]
    mixed = side_by_side(to_owners(mixed_all.reshape(count, tok_rows, own_cols)))
    mixed = mixed.astype(jnp.float32) + skip * ssm_input.astype(jnp.float32)
    gate = ssm_gate.astype(jnp.float32)
    sigmoid = jax.nn.sigmoid(gate)
    gated = mixed * gate * sigmoid
    d_normed = ssm_cotangent.astype(jnp.float32) * norm_gain
    sums = lax.psum(
        jnp.stack([jnp.sum(gated * gated, axis=1), jnp.sum(d_normed * gated, axis=1)]), "tp"
    )
    root_mean = jnp.sqrt(sums[0] / CH + EPSILON)[:, None]
    inner_mean = (sums[1] / CH)[:, None] / root_mean
    normed = gated / root_mean
    ssm_output = (normed * norm_gain).astype(jnp.bfloat16)
    d_gated = (d_normed - normed * inner_mean) / root_mean
    d_mixed = d_gated * gate * sigmoid
    gate_grad = (d_gated * mixed * sigmoid * (1.0 + gate * (1.0 - sigmoid))).astype(jnp.bfloat16)
    d_mixed_short, kv_all = lax.optimization_barrier((d_mixed.astype(jnp.bfloat16), kv_all))
    attn_output, query_grad, dkv = attention_core(
        queries, kv_all, attn_cotangent, lax.axis_index("ctx")
    )
    dm_all = to_channels(d_mixed_short).reshape(*folded, own_cols)
    dkv, dm_all = lax.optimization_barrier((dkv, dm_all))
    key_grad, value_grad = scatter_pair(dkv)
    input_all, write_all, read_all = scan_backward(
        x_all, dm_all, b_all, c_all, col, row, state_all
    )
    blocks = (count, tok_rows)
    input_all = input_all.reshape(*blocks, own_cols)
    write_all, read_all = write_all.reshape(*blocks, states), read_all.reshape(*blocks, states)
    if share_maps:
        kept = jnp.where(first, write_all, read_all)
        passed = from_other_core(jnp.where(first, read_all, write_all))
        maps_all = (kept.astype(jnp.float32) + passed.astype(jnp.float32)).astype(jnp.bfloat16)
    else:
        maps_all = jnp.concatenate([write_all, read_all], axis=2)
    back = to_owners(jnp.concatenate([input_all, maps_all], axis=2))
    input_g = side_by_side(back[:, :, :own_cols]).astype(jnp.float32)
    input_grad = (input_g + skip * d_mixed).astype(jnp.bfloat16)
    maps = jnp.sum(back[:, :, own_cols:].astype(jnp.float32), axis=0)
    if share_maps:
        other = from_other_core(maps)
        write_grad, read_grad = jnp.where(first, maps, other), jnp.where(first, other, maps)
    else:
        maps = lax.psum(maps.astype(jnp.bfloat16), "tp").astype(jnp.float32)
        write_grad, read_grad = maps[:, :states], maps[:, states:]
    return (
        ssm_output, input_grad, gate_grad, write_grad, read_grad,
        attn_output, query_grad, key_grad, value_grad,
    )


def solution(mesh):
    placed = (
        P("ctx", "tp"),
        P("ctx", "tp"),
        P("ctx", None),
        P("ctx", None),
        P("ctx", "tp"),
        P("tp"),
        P("tp"),
        P("ctx", "tp"),
        P("ctx", "tp"),
        P("ctx", "tp"),
        P("ctx", "tp"),
        P("ctx", "tp"),
    )
    return jax.shard_map(
        both_layers,
        mesh=mesh,
        in_specs=placed,
        out_specs=(
            P("ctx", "tp"),
            P("ctx", "tp"),
            P("ctx", "tp"),
            P("ctx", None),
            P("ctx", None),
            P("ctx", "tp"),
            P("ctx", "tp"),
            P("ctx", "tp"),
            P("ctx", "tp"),
        ),
        check_vma=False,
    )
```

```python
import functools

import jax
import jax.numpy as jnp
from jax import lax
from jax.experimental import pallas as pl
from jax.experimental.pallas import tpu as pltpu
from jax.sharding import PartitionSpec as P

HD = 128
CH = 8192
PRECISE = lax.Precision.HIGHEST
NEGATIVE = -1e30
EPSILON = 1e-05
TILE_KEYS = 256
CHUNK = 256
VMEM_BYTES = 48 * 1024 * 1024


def dot(a, b, a_dim, b_dim):
    return lax.dot_general(
        a, b, (((a_dim,), (b_dim,)), ((), ())), preferred_element_type=jnp.float32
    )


def attention_kernel(
    place_ref, q_ref, kv_ref, cot_ref, out_ref, dq_ref, dkv_ref,
    keys, values, dk_sum, dv_sum, scores, q_rows, cot_rows, acc,
):
    count, _, _, half_rows, _ = kv_ref.shape
    group = q_ref.shape[1] // HD
    rows = group * half_rows
    scale = HD ** (-0.5)
    place = place_ref[0]
    for j in range(count):
        near = pl.ds(j * half_rows, half_rows)
        far = pl.ds((2 * count - 1 - j) * half_rows, half_rows)
        keys[near] = kv_ref[j, 0, 0]
        keys[far] = kv_ref[j, 0, 1]
        values[near] = kv_ref[j, 1, 0]
        values[far] = kv_ref[j, 1, 1]
    dk_sum[...] = jnp.zeros_like(dk_sum)
    dv_sum[...] = jnp.zeros_like(dv_sum)
    for half in range(2):
        block = place if half == 0 else 2 * count - 1 - place
        tiles = block // (TILE_KEYS // half_rows) + 1
        for h in range(group):
            there = (pl.ds(half * half_rows, half_rows), pl.ds(h * HD, HD))
            q_rows[pl.ds(h * half_rows, half_rows)] = q_ref[there]
            cot_rows[pl.ds(h * half_rows, half_rows)] = cot_ref[there]
        q_pos = block * half_rows + lax.broadcasted_iota(jnp.int32, (1, rows), 1) % half_rows

        def score_turn(tile, top):
            at = pl.ds(pl.multiple_of(tile * TILE_KEYS, TILE_KEYS), TILE_KEYS)
            s = dot(keys[at], q_rows[...], 1, 1) * scale
            key_pos = tile * TILE_KEYS + lax.broadcasted_iota(jnp.int32, s.shape, 0)
            s = jnp.where(key_pos <= q_pos, s, NEGATIVE)
            scores[at] = s
            return jnp.maximum(top, jnp.max(s, axis=0, keepdims=True))

        top = lax.fori_loop(0, tiles, score_turn, jnp.full((1, rows), NEGATIVE, jnp.float32))
        acc[...] = jnp.zeros_like(acc)

        def value_turn(tile, total):
            at = pl.ds(pl.multiple_of(tile * TILE_KEYS, TILE_KEYS), TILE_KEYS)
            p = jnp.exp(scores[at] - top)
            scores[at] = p
            acc[...] += dot(values[at], p.astype(jnp.bfloat16), 0, 0)
            return total + jnp.sum(p, axis=0, keepdims=True)

        total = lax.fori_loop(0, tiles, value_turn, jnp.zeros((1, rows), jnp.float32))
        inverse = 1.0 / total
        out_t = acc[...] * inverse
        out_rows = out_t.T.astype(jnp.bfloat16)
        cot_t = cot_rows[...].astype(jnp.float32).T
        delta = jnp.sum(
            cot_t * out_t.astype(jnp.bfloat16).astype(jnp.float32), axis=0, keepdims=True
        )
        acc[...] = jnp.zeros_like(acc)

        def grad_turn(tile, carry):
            at = pl.ds(pl.multiple_of(tile * TILE_KEYS, TILE_KEYS), TILE_KEYS)
            w = scores[at] * inverse
            d_prob = dot(values[at], cot_rows[...], 1, 1)
            d_score = (w * (d_prob - delta) * scale).astype(jnp.bfloat16)
            acc[...] += dot(keys[at], d_score, 0, 0)
            dk_sum[at] += dot(d_score, q_rows[...], 1, 0)
            dv_sum[at] += dot(w.astype(jnp.bfloat16), cot_rows[...], 1, 0)
            return carry

        lax.fori_loop(0, tiles, grad_turn, 0)
        dq_rows = acc[...].T.astype(jnp.bfloat16)
        for h in range(group):
            there = (pl.ds(half * half_rows, half_rows), pl.ds(h * HD, HD))
            out_ref[there] = out_rows[h * half_rows : (h + 1) * half_rows]
            dq_ref[there] = dq_rows[h * half_rows : (h + 1) * half_rows]
    for j in range(count):
        near = pl.ds(j * half_rows, half_rows)
        far = pl.ds((2 * count - 1 - j) * half_rows, half_rows)
        dkv_ref[j, 0, 0] = dk_sum[near].astype(jnp.bfloat16)
        dkv_ref[j, 0, 1] = dk_sum[far].astype(jnp.bfloat16)
        dkv_ref[j, 1, 0] = dv_sum[near].astype(jnp.bfloat16)
        dkv_ref[j, 1, 1] = dv_sum[far].astype(jnp.bfloat16)


def attention_core(queries, kv_all, attn_cotangent, place):
    tok_rows, q_cols = queries.shape
    count, _, _, half_rows, kv_cols = kv_all.shape
    kv_heads = kv_cols // HD
    width = q_cols // kv_heads
    rows = width // HD * half_rows
    total = count * tok_rows
    wide = pl.BlockSpec((tok_rows, width), lambda g, place: (0, g))
    pair = pl.BlockSpec((count, 2, 2, half_rows, HD), lambda g, place: (0, 0, 0, 0, g))
    like_q = jax.ShapeDtypeStruct(queries.shape, jnp.bfloat16)
    flops = 7 * 2 * tok_rows * q_cols * total // 2
    return pl.pallas_call(
        attention_kernel,
        out_shape=(like_q, like_q, jax.ShapeDtypeStruct(kv_all.shape, jnp.bfloat16)),
        grid_spec=pltpu.PrefetchScalarGridSpec(
            num_scalar_prefetch=1,
            grid=(kv_heads,),
            in_specs=[wide, pair, wide],
            out_specs=(wide, wide, pair),
            scratch_shapes=[
                pltpu.VMEM((total, HD), jnp.bfloat16),
                pltpu.VMEM((total, HD), jnp.bfloat16),
                pltpu.VMEM((total, HD), jnp.float32),
                pltpu.VMEM((total, HD), jnp.float32),
                pltpu.VMEM((total, rows), jnp.float32),
                pltpu.VMEM((rows, HD), jnp.bfloat16),
                pltpu.VMEM((rows, HD), jnp.bfloat16),
                pltpu.VMEM((HD, rows), jnp.float32),
            ],
        ),
        compiler_params=pltpu.CompilerParams(vmem_limit_bytes=VMEM_BYTES),
        cost_estimate=pl.CostEstimate(
            flops=3 * flops, bytes_accessed=16 * 1024 * 1024, transcendentals=total * q_cols // 2
        ),
        name="attention_both",
    )(place.reshape(1).astype(jnp.int32), queries, kv_all, attn_cotangent)


def gather_pair(kv):
    _, tok_rows, kv_cols = kv.shape
    return lax.all_gather(kv, "ctx", axis=0).reshape(
        lax.axis_size("ctx"), 2, 2, tok_rows // 2, kv_cols
    )


def scatter_pair(dkv):
    count, _, _, half_rows, kv_cols = dkv.shape
    mine = lax.psum_scatter(
        dkv.reshape(count, 2, 2 * half_rows, kv_cols), "ctx", scatter_dimension=0, tiled=False
    )
    return (mine[0], mine[1])


def in_order(ref, step, steps):
    pieces = ref.shape[0]
    early = step < steps // 2
    return [ref[jnp.where(early, j, pieces - 1 - j)] for j in range(pieces)]


def put_in_order(ref, value, step, steps):
    pieces, rows = ref.shape[0], ref.shape[1]
    early = step < steps // 2
    for j in range(pieces):
        ref[jnp.where(early, j, pieces - 1 - j)] = value[j * rows : (j + 1) * rows].astype(
            ref.dtype
        )


def whole(ref, step, steps):
    return jnp.concatenate(in_order(ref, step, steps), axis=0)


def causal_decay(col, row, flip):
    shape = (col.shape[0], row.shape[1])
    down = lax.broadcasted_iota(jnp.int32, shape, 0)
    across = lax.broadcasted_iota(jnp.int32, shape, 1)
    if flip:
        return jnp.exp(jnp.where(across >= down, row - col, NEGATIVE))
    return jnp.exp(jnp.where(down >= across, col - row, NEGATIVE))


def forward_kernel(steps, x_ref, b_ref, c_ref, col_ref, row_ref, mixed_ref, state_ref, state):
    step = pl.program_id(0)

    @pl.when(step == 0)
    def _():
        state[...] = jnp.zeros_like(state)

    x = whole(x_ref, step, steps)
    b = whole(b_ref, step, steps)
    c = whole(c_ref, step, steps)
    col, row = col_ref[...], row_ref[0]
    last = col[CHUNK - 1 : CHUNK]
    weights = (causal_decay(col, row, False) * dot(c, b, 1, 1)).astype(jnp.bfloat16)
    entering = state[...]
    entering_short = entering.astype(jnp.bfloat16)
    state_ref[0] = entering_short
    mixed = dot(weights, x, 1, 0) + jnp.exp(col) * dot(c, entering_short, 1, 0)
    put_in_order(mixed_ref, mixed, step, steps)
    shrunk = (b.astype(jnp.float32) * jnp.exp(last - col)).astype(jnp.bfloat16)
    state[...] = jnp.exp(last) * entering + dot(shrunk, x, 0, 0)


def backward_kernel(
    steps, x_ref, dm_ref, b_ref, c_ref, col_ref, row_ref, state_ref,
    input_ref, write_ref, read_ref, adjoint,
):
    step = steps - 1 - pl.program_id(0)

    @pl.when(pl.program_id(0) == 0)
    def _():
        adjoint[...] = jnp.zeros_like(adjoint)

    x = whole(x_ref, step, steps)
    dm = whole(dm_ref, step, steps)
    b = whole(b_ref, step, steps)
    c = whole(c_ref, step, steps)
    col, row = col_ref[...], row_ref[0]
    last = col[CHUNK - 1 : CHUNK]
    shrink, grow = jnp.exp(last - col), jnp.exp(col)
    entering = adjoint[...]
    entering_short = entering.astype(jnp.bfloat16)
    decay_t = causal_decay(col, row, True)
    weights_t = (decay_t * dot(b, c, 1, 1)).astype(jnp.bfloat16)
    input_g = dot(weights_t, dm, 1, 0) + shrink * dot(b, entering_short, 1, 0)
    put_in_order(input_ref, input_g, step, steps)
    pairs_t = (decay_t * dot(x, dm, 1, 1)).astype(jnp.bfloat16)
    write_g = dot(pairs_t, c, 1, 0) + shrink * dot(x, entering_short, 1, 1)
    pairs = (causal_decay(col, row, False) * dot(dm, x, 1, 1)).astype(jnp.bfloat16)
    read_g = dot(pairs, b, 1, 0) + grow * dot(dm, state_ref[0], 1, 1)
    put_in_order(write_ref, write_g, step, steps)
    put_in_order(read_ref, read_g, step, steps)
    grown = (c.astype(jnp.float32) * grow).astype(jnp.bfloat16)
    adjoint[...] = jnp.exp(last) * entering + dot(grown, dm, 0, 0)


def ssm_specs(count, half_rows, steps, order):
    per = CHUNK // half_rows

    def rows_spec(cols):
        def place(i):
            step = order(i)
            early = step < steps // 2
            return (
                jnp.where(early, step, steps - 1 - step), jnp.where(early, 0, 1), 0, 0
            )

        return pl.BlockSpec((per, pl.Squeezed(), half_rows, cols), place)

    return (
        rows_spec,
        pl.BlockSpec((CHUNK, 1), lambda i: (order(i), 0)),
        pl.BlockSpec((1, 1, CHUNK), lambda i: (order(i), 0, 0)),
    )


def scan_forward(x, b, c, col, row):
    count, _, half_rows, cols = x.shape
    states = b.shape[-1]
    steps = count * 2 * half_rows // CHUNK
    rows_spec, col_spec, row_spec = ssm_specs(count, half_rows, steps, lambda i: i)
    return pl.pallas_call(
        functools.partial(forward_kernel, steps),
        grid=(steps,),
        in_specs=[rows_spec(cols), rows_spec(states), rows_spec(states), col_spec, row_spec],
        out_specs=(rows_spec(cols), pl.BlockSpec((1, states, cols), lambda i: (i, 0, 0))),
        out_shape=(
            jax.ShapeDtypeStruct(x.shape, jnp.bfloat16),
            jax.ShapeDtypeStruct((steps, states, cols), jnp.bfloat16),
        ),
        scratch_shapes=[pltpu.VMEM((states, cols), jnp.float32)],
        compiler_params=pltpu.CompilerParams(vmem_limit_bytes=VMEM_BYTES),
        cost_estimate=pl.CostEstimate(
            flops=10**9, bytes_accessed=6 * 1024 * 1024, transcendentals=5 * 10**5
        ),
        name="scan_forward",
    )(x, b, c, col, row)


def scan_backward(x, dm, b, c, col, row, state):
    count, _, half_rows, cols = x.shape
    states = b.shape[-1]
    steps = count * 2 * half_rows // CHUNK
    rows_spec, col_spec, row_spec = ssm_specs(
        count, half_rows, steps, lambda i: steps - 1 - i
    )
    return pl.pallas_call(
        functools.partial(backward_kernel, steps),
        grid=(steps,),
        in_specs=[
            rows_spec(cols), rows_spec(cols), rows_spec(states), rows_spec(states),
            col_spec, row_spec,
            pl.BlockSpec((1, states, cols), lambda i: (steps - 1 - i, 0, 0)),
        ],
        out_specs=(rows_spec(cols), rows_spec(states), rows_spec(states)),
        out_shape=(
            jax.ShapeDtypeStruct(x.shape, jnp.bfloat16),
            jax.ShapeDtypeStruct(b.shape, jnp.bfloat16),
            jax.ShapeDtypeStruct(b.shape, jnp.bfloat16),
        ),
        scratch_shapes=[pltpu.VMEM((states, cols), jnp.float32)],
        compiler_params=pltpu.CompilerParams(vmem_limit_bytes=VMEM_BYTES),
        cost_estimate=pl.CostEstimate(
            flops=2 * 10**9, bytes_accessed=6 * 1024 * 1024, transcendentals=10**6
        ),
        name="scan_backward",
    )(x, dm, b, c, col, row, state)


def to_channels(values, extra=None):
    count = lax.axis_size("ctx")
    parts = values.reshape(values.shape[0], count, -1)
    if extra is not None:
        shape = (values.shape[0], count, extra.shape[1])
        parts = jnp.concatenate([parts, jnp.broadcast_to(extra[:, None, :], shape)], axis=2)
    blocks = jnp.transpose(parts, (1, 0, 2))
    return lax.all_to_all(blocks, "ctx", split_axis=0, concat_axis=0)


def to_owners(blocks):
    return lax.all_to_all(blocks, "ctx", split_axis=0, concat_axis=0)


def side_by_side(blocks):
    return jnp.transpose(blocks, (1, 0, 2)).reshape(blocks.shape[1], -1)


def from_other_core(values):
    return lax.ppermute(values, "tp", [(0, 1), (1, 0)])


def both_layers(
    ssm_input, ssm_gate, state_write, state_read, log_decay, skip_gain, norm_gain, ssm_cotangent,
    queries, key_states, value_states, attn_cotangent,
):
    tok_rows, channel_count = ssm_input.shape
    head_count = log_decay.shape[1]
    half_rows = tok_rows // 2
    head_dim = channel_count // head_count
    count = lax.axis_size("ctx")
    own_cols = channel_count // count
    states = state_write.shape[1]
    folded = (count, 2, half_rows)
    share_maps = lax.axis_size("tp") == 2
    kv = jnp.stack([key_states, value_states])
    kv, sent_input, log_decay = lax.optimization_barrier((kv, ssm_input, log_decay))
    kv_all = gather_pair(kv)
    if share_maps:
        first = lax.axis_index("tp") == 0
        arrived = to_channels(sent_input, jnp.where(first, state_write, state_read))
        own_map = arrived[:, :, own_cols:]
        other_map = from_other_core(own_map)
        b_all = jnp.where(first, own_map, other_map).reshape(*folded, states)
        c_all = jnp.where(first, other_map, own_map).reshape(*folded, states)
    else:
        arrived = to_channels(sent_input, jnp.concatenate([state_write, state_read], axis=1))
        b_all = arrived[:, :, own_cols : own_cols + states].reshape(*folded, states)
        c_all = arrived[:, :, own_cols + states :].reshape(*folded, states)
    x_all = arrived[:, :, :own_cols].reshape(*folded, own_cols)
    decay_rows = jnp.repeat(log_decay.T, head_dim // own_cols, axis=0)
    own_decay = to_owners(decay_rows[:, None, :]).reshape(*folded)
    ordered = jnp.concatenate([own_decay[:, 0], own_decay[::-1, 1]]).reshape(-1, CHUNK)
    upto = jnp.triu(jnp.ones((CHUNK, CHUNK), jnp.float32))
    log_total = jnp.dot(ordered, upto, precision=PRECISE)
    col = log_total.reshape(-1, 1)
    row = log_total[:, None, :]
    mixed_all, state_all = scan_forward(x_all, b_all, c_all, col, row)
    mixed_all, kv_all = lax.optimization_barrier((mixed_all, kv_all))
    attn_output, query_grad, dkv = attention_core(
        queries, kv_all, attn_cotangent, lax.axis_index("ctx")
    )
    mixed_back = to_owners(mixed_all.reshape(count, tok_rows, own_cols))
    dkv, mixed_back = lax.optimization_barrier((dkv, mixed_back))
    key_grad, value_grad = scatter_pair(dkv)
    skip = jnp.repeat(skip_gain, head_dim)[None, :]
    mixed = side_by_side(mixed_back)
    mixed = mixed.astype(jnp.float32) + skip * ssm_input.astype(jnp.float32)
    gate = ssm_gate.astype(jnp.float32)
    sigmoid = jax.nn.sigmoid(gate)
    gated = mixed * gate * sigmoid
    d_normed = ssm_cotangent.astype(jnp.float32) * norm_gain
    sums = lax.psum(
        jnp.stack([jnp.sum(gated * gated, axis=1), jnp.sum(d_normed * gated, axis=1)]), "tp"
    )
    root_mean = jnp.sqrt(sums[0] / CH + EPSILON)[:, None]
    inner_mean = (sums[1] / CH)[:, None] / root_mean
    normed = gated / root_mean
    ssm_output = (normed * norm_gain).astype(jnp.bfloat16)
    d_gated = (d_normed - normed * inner_mean) / root_mean
    d_mixed = d_gated * gate * sigmoid
    gate_grad = (d_gated * mixed * sigmoid * (1.0 + gate * (1.0 - sigmoid))).astype(jnp.bfloat16)
    dm_all = to_channels(d_mixed.astype(jnp.bfloat16)).reshape(*folded, own_cols)
    input_all, write_all, read_all = scan_backward(
        x_all, dm_all, b_all, c_all, col, row, state_all
    )
    blocks = (count, tok_rows)
    input_all = input_all.reshape(*blocks, own_cols)
    write_all, read_all = write_all.reshape(*blocks, states), read_all.reshape(*blocks, states)
    if share_maps:
        kept = jnp.where(first, write_all, read_all)
        passed = from_other_core(jnp.where(first, read_all, write_all))
        maps_all = (kept.astype(jnp.float32) + passed.astype(jnp.float32)).astype(jnp.bfloat16)
    else:
        maps_all = jnp.concatenate([write_all, read_all], axis=2)
    back = to_owners(jnp.concatenate([input_all, maps_all], axis=2))
    input_g = side_by_side(back[:, :, :own_cols]).astype(jnp.float32)
    input_grad = (input_g + skip * d_mixed).astype(jnp.bfloat16)
    maps = jnp.sum(back[:, :, own_cols:].astype(jnp.float32), axis=0)
    if share_maps:
        other = from_other_core(maps)
        write_grad, read_grad = jnp.where(first, maps, other), jnp.where(first, other, maps)
    else:
        maps = lax.psum(maps.astype(jnp.bfloat16), "tp").astype(jnp.float32)
        write_grad, read_grad = maps[:, :states], maps[:, states:]
    return (
        ssm_output, input_grad, gate_grad, write_grad, read_grad,
        attn_output, query_grad, key_grad, value_grad,
    )


def solution(mesh):
    placed = (
        P("ctx", "tp"),
        P("ctx", "tp"),
        P("ctx", None),
        P("ctx", None),
        P("ctx", "tp"),
        P("tp"),
        P("tp"),
        P("ctx", "tp"),
        P("ctx", "tp"),
        P("ctx", "tp"),
        P("ctx", "tp"),
        P("ctx", "tp"),
    )
    return jax.shard_map(
        both_layers,
        mesh=mesh,
        in_specs=placed,
        out_specs=(
            P("ctx", "tp"),
            P("ctx", "tp"),
            P("ctx", "tp"),
            P("ctx", None),
            P("ctx", None),
            P("ctx", "tp"),
            P("ctx", "tp"),
            P("ctx", "tp"),
            P("ctx", "tp"),
        ),
        check_vma=False,
    )
```
